32 devices in a mesh: seq: 8 (over z, y), dp: 4 (over x, core).
Axes of the slice: x: 2, y: 2, z: 4, core: 2. Of those that a mesh axis runs over, the one named last changes fastest.
Arguments:
- queries: bfloat16 [4, 512, 1024], P('dp', 'seq'), may hold values from -8 to 8
- key_rows: bfloat16 [4, 512, 1024], P('dp', 'seq'), may hold values from -8 to 8
- value_rows: bfloat16 [4, 512, 1024], P('dp', 'seq'), may hold values from -6 to 6
- out_grad: bfloat16 [4, 512, 1024], P('dp', 'seq'), may hold values from -16 to 16
- mem_keys: bfloat16 [4, 1024, 1024], P('dp', 'seq'), may hold values from -6 to 6
- mem_values: bfloat16 [4, 1024, 1024], P('dp', 'seq'), may hold values from -6 to 6
- content_bias: float32 [8, 128], P('seq'), may hold values from -3 to 3
- passage_ids: int32 [4, 512], P('dp'), may hold values from 0 to 8, as said below
Outputs:
- d_queries: bfloat16 [4, 512, 1024], P('dp', 'seq')
- d_keys: bfloat16 [4, 512, 1024], P('dp', 'seq')
- d_values: bfloat16 [4, 512, 1024], P('dp', 'seq')
- d_bias: float32 [8, 128], P('seq')
The draws below stay inside these ranges and needn't reach their ends.
Inputs may be any that keep to these rules, and one draw needn't show every extreme that they name: `passage_ids`: ids never fall along a sequence. Exactly one new passage starts in each aligned block of 64 positions, never at position 0, so passage 0 is not empty. A passage holds at most 127 positions, and some passage of every sequence holds exactly that many.
All inputs are finite; a program needn't handle non-finite values.
Results may differ from the reference program's by a relative error of at most 0.012.
The reference program's roundings to bfloat16 on the way (of `shifted`, `weights_bf` and `score_grad`) count: a program that leaves them out, or rounds other values in their place, can miss the bound.
Values may be sent and summed in bfloat16 or wider, within the bound.
No kernel may reach another device: no remote copies, remote signals or barrier semaphores. Data moves between devices by JAX's collectives and lax.ppermute only.
A program may use at most 64 MiB of HBM per device.

```python
import math
import jax
import jax.numpy as jnp
from jax import lax

HEAD = 128
TOK_DEV = 64
MEM_ROWS = 1024
HEADS = 8
D = 1024
L = 512
SEQS = 4
PASSAGES = 8
BLOCK_ROWS = 512


def passage_starts(key):
    base = jax.random.fold_in(key, 7)
    offsets = jax.random.randint(jax.random.fold_in(base, 1), (SEQS, PASSAGES), 0, TOK_DEV)
    first = jax.random.randint(jax.random.fold_in(base, 2), (SEQS, 1), 1, TOK_DEV)
    longest = jax.random.randint(jax.random.fold_in(base, 3), (SEQS, 1), 1, PASSAGES - 1)
    column = jnp.arange(PASSAGES, dtype=jnp.int32)[None, :]
    offsets = jnp.where(column == 0, first, offsets)
    offsets = jnp.where(column == longest, 0, jnp.where(column == longest + 1, TOK_DEV - 1, offsets))
    return (column * TOK_DEV + offsets).astype(jnp.int32)


def draw_passage_ids(key, part):
    starts = passage_starts(key)
    position = jnp.arange(L, dtype=jnp.int32)
    return jnp.sum((starts[:, None, :] <= position[None, :, None]).astype(jnp.int32), axis=2).astype(jnp.int32)


def query_key_pair(key):
    shape = (SEQS, L, D)
    query_draw = jnp.clip(jax.random.normal(jax.random.fold_in(key, 23), shape, jnp.float32), -4.0, 4.0)
    key_draw = jnp.clip(jax.random.normal(jax.random.fold_in(key, 24), shape, jnp.float32), -4.0, 4.0)
    return (query_draw, key_draw)


def draw_queries(key, part):
    return query_key_pair(key)[0].astype(jnp.bfloat16)


def draw_key_rows(key, part):
    return query_key_pair(key)[1].astype(jnp.bfloat16)


def draw_out_grad(key, part):
    shape = (SEQS, L, D)
    seq_index = jnp.arange(SEQS).astype(jnp.float32)[:, None, None] / max(SEQS - 1, 1)
    base = jnp.clip(jax.random.normal(jax.random.fold_in(key, 31), shape, jnp.float32), -4.0, 4.0)
    rise = 3.0 ** seq_index
    return (base * rise).astype(jnp.bfloat16)


def block_levels(key, shape, cuts, low, largest):
    loudness = 1.0
    for dim, blocks in cuts:
        draws = jax.random.uniform(jax.random.fold_in(jax.random.fold_in(key, 6), dim), (blocks,), jnp.float32, low / len(cuts), largest / len(cuts))
        loudness = loudness * jnp.repeat(jnp.exp(draws), shape[dim] // blocks).reshape((-1,) + (1,) * (len(shape) - 1 - dim))
    return loudness


def bell_draw(own_key, shape, deviation, bound, pieces=(), held_as=jnp.bfloat16):
    values = deviation * jax.random.normal(own_key, shape, jnp.float32)
    if pieces:
        values = values * block_levels(own_key, shape, pieces, -0.22, 0.18)
    return jnp.clip(values, -bound, bound).astype(held_as)


def setup_inputs(seed: int = 0) -> dict:
    key_of = jax.random.split(jax.random.key(seed), 9)
    return {
        "queries": draw_queries(jax.random.fold_in(key_of[8], 71), 0),
        "key_rows": draw_key_rows(jax.random.fold_in(key_of[8], 71), 0),
        "value_rows": bell_draw(key_of[2], (SEQS, L, D), 1.0, 6.0, ((0, 4), (1, 8))),
        "out_grad": draw_out_grad(jax.random.fold_in(key_of[8], 71), 0),
        "mem_keys": bell_draw(key_of[4], (SEQS, MEM_ROWS, D), 1.0, 6.0, ((0, 4), (1, 8))),
        "mem_values": bell_draw(key_of[5], (SEQS, MEM_ROWS, D), 1.0, 6.0, ((0, 4), (1, 8))),
        "content_bias": bell_draw(key_of[6], (HEADS, HEAD), 0.5, 3.0, ((0, 8),), jnp.float32),
        "passage_ids": draw_passage_ids(jax.random.fold_in(key_of[8], 71), 0),
    }


def accumulate(total, part, begin):
    current = lax.dynamic_slice_in_dim(total, begin, part.shape[0], 0)
    return lax.dynamic_update_slice_in_dim(total, current + part, begin, 0)

def padded(key_head, value_head, passages, reach_back):
    zeros = jnp.zeros((reach_back, key_head.shape[1]), key_head.dtype)
    keys_pad = jnp.concatenate([zeros, key_head], axis=0)
    values_pad = jnp.concatenate([zeros, value_head], axis=0)
    passage_pad = jnp.concatenate([jnp.full((reach_back,), -1, jnp.int32), passages.astype(jnp.int32)], axis=0)
    return (keys_pad, values_pad, passage_pad)

def block_weights(begin, prepared, passages, reach_back, block_rows, scale):
    shifted, keys_pad, values_pad, passage_pad, mem_k, mem_v = prepared
    query_blk = lax.dynamic_slice_in_dim(shifted, begin, block_rows, 0)
    local_keys = lax.dynamic_slice_in_dim(keys_pad, begin, reach_back + block_rows, 0)
    local_values = lax.dynamic_slice_in_dim(values_pad, begin, reach_back + block_rows, 0)
    key_all = jnp.concatenate([mem_k, local_keys], axis=0)
    value_all = jnp.concatenate([mem_v, local_values], axis=0)
    query_pass = lax.dynamic_slice_in_dim(passages, begin, block_rows, 0)
    key_pass = lax.dynamic_slice_in_dim(passage_pad, begin, reach_back + block_rows, 0)
    query_pos = begin + jnp.arange(block_rows, dtype=jnp.int32)
    key_pos = begin - reach_back + jnp.arange(reach_back + block_rows, dtype=jnp.int32)
    local_seen = (key_pos[None, :] <= query_pos[:, None]) & (key_pass[None, :] == query_pass[:, None])
    memory_seen = jnp.ones((block_rows, mem_k.shape[0]), dtype=bool)
    seen = jnp.concatenate([memory_seen, local_seen], axis=1)
    raw = lax.dot_general(query_blk, key_all, (((1,), (1,)), ((), ())), preferred_element_type=jnp.float32) * scale
    scores = jnp.where(seen, raw, -jnp.inf)
    top = lax.optimization_barrier(jnp.max(scores, axis=1, keepdims=True))
    expo = jnp.where(seen, jnp.exp(scores - top), 0.0)
    weights = expo / lax.optimization_barrier(jnp.sum(expo, axis=1, keepdims=True))
    return (query_blk, key_all, value_all, weights, weights.astype(jnp.bfloat16))

def block_grads(query_blk, key_all, value_all, weights, weights_bf, attended, grad_blk, mem_rows, scale):
    delta = lax.optimization_barrier(jnp.sum(grad_blk.astype(jnp.float32) * attended, axis=1, keepdims=True))
    value_dots = lax.dot_general(grad_blk, value_all, (((1,), (1,)), ((), ())), preferred_element_type=jnp.float32)
    score_grad = (weights * (value_dots - delta) * scale).astype(jnp.bfloat16)
    query_grad = jnp.dot(score_grad, key_all, preferred_element_type=jnp.float32)
    key_grad = lax.dot_general(score_grad[:, mem_rows:], query_blk, (((0,), (0,)), ((), ())), preferred_element_type=jnp.float32)
    value_grad = lax.dot_general(weights_bf[:, mem_rows:], grad_blk, (((0,), (0,)), ((), ())), preferred_element_type=jnp.float32)
    return (query_grad, key_grad, value_grad)

def gradient_pass(prepared, passages, reach_back, block_rows, grad_head):
    shifted = prepared[0]
    mem_rows = prepared[4].shape[0]
    length, head_size = shifted.shape
    scale = 1.0 / math.sqrt(head_size)
    starts = jnp.arange(length // block_rows, dtype=jnp.int32) * block_rows

    def step(carry, begin):
        key_acc, value_acc = carry
        query_blk, key_all, value_all, weights, weights_bf = block_weights(begin, prepared, passages, reach_back, block_rows, scale)
        attended = jnp.dot(weights_bf, value_all, preferred_element_type=jnp.float32)
        grad_blk = lax.dynamic_slice_in_dim(grad_head, begin, block_rows, 0)
        query_grad, key_grad, value_grad = block_grads(query_blk, key_all, value_all, weights, weights_bf, attended, grad_blk, mem_rows, scale)
        return ((accumulate(key_acc, key_grad, begin), accumulate(value_acc, value_grad, begin)), query_grad)
    zeros = jnp.zeros((reach_back + length, head_size), jnp.float32)
    (key_acc, value_acc), query_parts = lax.scan(step, (zeros, zeros), starts)
    query_grad = query_parts.reshape(length, head_size)
    return (query_grad, key_acc[reach_back:].astype(jnp.bfloat16), value_acc[reach_back:].astype(jnp.bfloat16))

def reference(queries, key_rows, value_rows, out_grad, mem_keys, mem_values, content_bias, passage_ids):
    seqs, length, width = queries.shape
    heads, head_size = content_bias.shape

    def by_heads(array):
        return array.reshape(array.shape[0], array.shape[1], heads, head_size).transpose(0, 2, 1, 3)
    shifted_all = (by_heads(queries).astype(jnp.float32) + content_bias[None, :, None, :]).astype(jnp.bfloat16)
    key_split = by_heads(key_rows)
    value_split = by_heads(value_rows)
    grad_split = by_heads(out_grad)
    memk_split = by_heads(mem_keys)
    memv_split = by_heads(mem_values)
    reach_back = 2 * TOK_DEV

    def per_item(item_index):
        seq_index = item_index // heads
        head_index = item_index % heads
        passages = passage_ids[seq_index]
        keys_pad, values_pad, passage_pad = padded(key_split[seq_index, head_index], value_split[seq_index, head_index], passages, reach_back)
        prepared = (shifted_all[seq_index, head_index], keys_pad, values_pad, passage_pad, memk_split[seq_index, head_index], memv_split[seq_index, head_index])
        query_grad, key_grad, value_grad = gradient_pass(prepared, passages, reach_back, BLOCK_ROWS, grad_split[seq_index, head_index])
        return (query_grad.astype(jnp.bfloat16), lax.optimization_barrier(jnp.sum(query_grad, axis=0)), key_grad, value_grad)
    items = jnp.arange(seqs * heads, dtype=jnp.int32)
    dq_all, bias_terms, dk_all, dv_all = lax.map(per_item, items)

    def merge_back(array):
        return array.reshape(seqs, heads, length, head_size).transpose(0, 2, 1, 3).reshape(seqs, length, width)
    d_bias = lax.optimization_barrier(jnp.sum(bias_terms.reshape(seqs, heads, head_size), axis=0)) / length
    return (merge_back(dq_all), merge_back(dk_all), merge_back(dv_all), d_bias)
```

```python
import functools
import math

import jax
import jax.numpy as jnp
from jax import lax
from jax.experimental import pallas as pl
from jax.experimental.pallas import tpu as pltpu
from jax.sharding import PartitionSpec as P

LOG2E = 1.4426950408889634
VMEM = pltpu.VMEM


def pack_kernel(n, width, *refs):
    ins, out = refs[:-1], refs[-1]
    row = 0
    for ref in ins:
        rows = ref.shape[1]
        for h in range(n):
            out[h, row : row + rows, :] = ref[0, :, h * width : (h + 1) * width]
        row += rows


def pack(arrays, n, width):
    rows = sum(a.shape[1] for a in arrays)
    return pl.pallas_call(
        functools.partial(pack_kernel, n, width),
        out_shape=jax.ShapeDtypeStruct((n, rows, width), arrays[0].dtype),
        in_specs=[pl.BlockSpec(memory_space=VMEM)] * len(arrays),
        out_specs=pl.BlockSpec(memory_space=VMEM),
        name="pack",
    )(*arrays)


def unpack_kernel(n, width, x_ref, *outs):
    rows = outs[0].shape[1]
    for k, out in enumerate(outs):
        for h in range(n):
            out[0, :, h * width : (h + 1) * width] = x_ref[h, k * rows : (k + 1) * rows, :]


def unpack(x, count, n, width):
    rows = x.shape[1] // count
    shape = jax.ShapeDtypeStruct((1, rows, n * width), x.dtype)
    return pl.pallas_call(
        functools.partial(unpack_kernel, n, width),
        out_shape=(shape,) * count,
        in_specs=[pl.BlockSpec(memory_space=VMEM)],
        out_specs=(pl.BlockSpec(memory_space=VMEM),) * count,
        name="unpack",
    )(x)


def dot_t(a, b):
    return lax.dot_general(a, b, (((1,), (1,)), ((), ())), preferred_element_type=jnp.float32)


def t_dot(a, b):
    return lax.dot_general(a, b, (((0,), (0,)), ((), ())), preferred_element_type=jnp.float32)


def attention_kernel(tok, mem, x_ref, bias_ref, pass_ref, out_ref, dbias_ref, kpad, vpad, dk_acc, dv_acc):
    n, _, width = x_ref.shape
    length = n * tok
    step = 2 * tok
    scale = 1.0 / math.sqrt(width)
    zeros = jnp.zeros((step, width), kpad.dtype)
    kpad[0:step, :] = zeros
    vpad[0:step, :] = zeros
    for s in range(n):
        kpad[step + s * tok : step + (s + 1) * tok, :] = x_ref[s, 2 * tok : 3 * tok, :]
        vpad[step + s * tok : step + (s + 1) * tok, :] = x_ref[s, 3 * tok : 4 * tok, :]
    mem_k = x_ref[:, 4 * tok : 4 * tok + mem, :].reshape(n * mem, width)
    mem_v = x_ref[:, 4 * tok + mem : 4 * tok + 2 * mem, :].reshape(n * mem, width)
    dk_acc[...] = jnp.zeros_like(dk_acc)
    dv_acc[...] = jnp.zeros_like(dv_acc)
    bias = bias_ref[...]
    rows = lax.broadcasted_iota(jnp.int32, (step, step), 0)
    cols = lax.broadcasted_iota(jnp.int32, (step, step), 1)
    causal = cols <= rows
    total = jnp.zeros((1, width), jnp.float32)
    ids_before = jnp.full((step, step), -1, jnp.int32)
    for c in range(length // step):
        lo = c * step
        ids = jnp.broadcast_to(pass_ref[:, lo : lo + step], (step, step))
        ids_q = ids.T
        seen = jnp.concatenate([ids_q == ids_before, (ids_q == ids) & causal], axis=1)
        ids_before = ids
        q = jnp.concatenate([x_ref[2 * c, 0:tok, :], x_ref[2 * c + 1, 0:tok, :]], axis=0)
        g = jnp.concatenate([x_ref[2 * c, tok : 2 * tok, :], x_ref[2 * c + 1, tok : 2 * tok, :]], axis=0)
        q = (q.astype(jnp.float32) + bias).astype(jnp.bfloat16)
        k_loc = kpad[lo : lo + 2 * step, :]
        v_loc = vpad[lo : lo + 2 * step, :]
        raw_m = dot_t(q, mem_k)
        raw_l = jnp.where(seen, dot_t(q, k_loc), -jnp.inf)
        top = jnp.maximum(jnp.max(raw_m, axis=1, keepdims=True), jnp.max(raw_l, axis=1, keepdims=True))
        e_m = jnp.exp2((raw_m - top) * (scale * LOG2E))
        e_l = jnp.exp2((raw_l - top) * (scale * LOG2E))
        norm = jnp.sum(e_m, axis=1, keepdims=True) + jnp.sum(e_l, axis=1, keepdims=True)
        inv = 1.0 / norm
        w_m = e_m * inv
        w_l = e_l * inv
        wb_m = w_m.astype(jnp.bfloat16)
        wb_l = w_l.astype(jnp.bfloat16)
        vd_m = dot_t(g, mem_v)
        vd_l = dot_t(g, v_loc)
        delta = jnp.sum(wb_m.astype(jnp.float32) * vd_m, axis=1, keepdims=True) + jnp.sum(
            wb_l.astype(jnp.float32) * vd_l, axis=1, keepdims=True
        )
        ds_m = (w_m * (vd_m - delta) * scale).astype(jnp.bfloat16)
        ds_l = (w_l * (vd_l - delta) * scale).astype(jnp.bfloat16)
        dq = jnp.dot(ds_m, mem_k, preferred_element_type=jnp.float32) + jnp.dot(
            ds_l, k_loc, preferred_element_type=jnp.float32
        )
        total = total + jnp.sum(dq, axis=0, keepdims=True)
        dq = dq.astype(out_ref.dtype)
        out_ref[2 * c, 0:tok, :] = dq[:tok]
        out_ref[2 * c + 1, 0:tok, :] = dq[tok:]
        dk_acc[lo : lo + 2 * step, :] += t_dot(ds_l, q)
        dv_acc[lo : lo + 2 * step, :] += t_dot(wb_l, g)
    for s in range(n):
        lo = step + s * tok
        out_ref[s, tok : 2 * tok, :] = dk_acc[lo : lo + tok, :].astype(out_ref.dtype)
        out_ref[s, 2 * tok : 3 * tok, :] = dv_acc[lo : lo + tok, :].astype(out_ref.dtype)
    dbias_ref[...] = total / length


def attention(x, bias, passages, tok, mem):
    n, _, width = x.shape
    length = n * tok
    pad = length + 2 * tok
    flops = 2 * length * width * (3 * n * mem + 5 * 4 * tok)
    return pl.pallas_call(
        functools.partial(attention_kernel, tok, mem),
        out_shape=(
            jax.ShapeDtypeStruct((n, 3 * tok, width), x.dtype),
            jax.ShapeDtypeStruct((1, width), jnp.float32),
        ),
        in_specs=[pl.BlockSpec(memory_space=VMEM)] * 3,
        out_specs=(pl.BlockSpec(memory_space=VMEM),) * 2,
        scratch_shapes=[
            VMEM((pad, width), x.dtype),
            VMEM((pad, width), x.dtype),
            VMEM((pad, width), jnp.float32),
            VMEM((pad, width), jnp.float32),
        ],
        cost_estimate=pl.CostEstimate(
            flops=flops, bytes_accessed=x.size * 3, transcendentals=length * (n * mem + 4 * tok)
        ),
        name="attention",
    )(x, bias, passages)


def body(n, queries, key_rows, value_rows, out_grad, mem_keys, mem_values, content_bias, passage_ids):
    tok, mem = queries.shape[1], mem_keys.shape[1]
    width = content_bias.shape[1]
    sent = pack((queries, out_grad, key_rows, value_rows, mem_keys, mem_values), n, width)
    x = lax.all_to_all(sent, "seq", split_axis=0, concat_axis=0, tiled=True)
    grads, d_bias = attention(x, content_bias, passage_ids, tok, mem)
    grads = lax.all_to_all(grads, "seq", split_axis=0, concat_axis=0, tiled=True)
    d_queries, d_keys, d_values = unpack(grads, 3, n, width)
    return (d_queries, d_keys, d_values, lax.psum(d_bias, "dp"))


def solution(mesh):
    rows = P("dp", "seq", None)
    return jax.shard_map(
        functools.partial(body, mesh.shape["seq"]),
        mesh=mesh,
        in_specs=(rows,) * 6 + (P("seq", None), P("dp", None)),
        out_specs=(rows,) * 3 + (P("seq", None),),
        check_vma=False,
    )
```

```python
import functools
import math

import jax
import jax.numpy as jnp
from jax import lax
from jax.experimental import pallas as pl
from jax.experimental.pallas import tpu as pltpu
from jax.sharding import PartitionSpec as P

LOG2E = 1.4426950408889634
VMEM = pltpu.VMEM
MIB = 2**20


def offsets(n):
    return sorted(range(n), key=lambda o: (-o.bit_length(), o))


def in_vmem(x):
    return pltpu.with_memory_space_constraint(x, VMEM)


def exchange(chunks, n):
    return [
        chunk if o == 0 else lax.ppermute(chunk, "seq", [(s, s ^ o) for s in range(n)])
        for o, chunk in zip(offsets(n), chunks, strict=True)
    ]


def columns(n, o, width):
    head = lax.axis_index("seq") ^ o
    return pl.ds(pl.multiple_of(head * width, width), width)


def pack_kernel(n, count, *refs):
    ins, outs, sem = refs[:count], refs[count:-1], refs[-1]
    width = outs[0].shape[1]
    copies = []
    for o, out in zip(offsets(n), outs, strict=True):
        cols = columns(n, o, width)
        row = 0
        for ref in ins:
            rows = ref.shape[1]
            copies.append(pltpu.make_async_copy(ref.at[0, :, cols], out.at[row : row + rows, :], sem))
            row += rows
    for copy in copies:
        copy.start()
    for copy in copies:
        copy.wait()


def pack(arrays, n, width):
    rows = sum(a.shape[1] for a in arrays)
    return pl.pallas_call(
        functools.partial(pack_kernel, n, len(arrays)),
        out_shape=(VMEM((rows, width), arrays[0].dtype),) * n,
        in_specs=[pl.BlockSpec(memory_space=pl.ANY)] * len(arrays),
        out_specs=(pl.BlockSpec(memory_space=VMEM),) * n,
        scratch_shapes=[pltpu.SemaphoreType.DMA],
        compiler_params=pltpu.CompilerParams(vmem_limit_bytes=8 * MIB),
        name="pack",
    )(*arrays)


def unpack_kernel(n, count, *refs):
    ins, outs, sem = refs[:n], refs[n:-1], refs[-1]
    width = ins[0].shape[1]
    rows = outs[0].shape[1]
    copies = []
    for o, ref in zip(offsets(n), ins, strict=True):
        cols = columns(n, o, width)
        for k, out in enumerate(outs):
            copies.append(pltpu.make_async_copy(ref.at[k * rows : (k + 1) * rows, :], out.at[0, :, cols], sem))
    for copy in copies:
        copy.start()
    for copy in copies:
        copy.wait()


def unpack(chunks, count, n, width):
    rows = chunks[0].shape[0] // count
    shape = jax.ShapeDtypeStruct((1, rows, n * width), chunks[0].dtype)
    return pl.pallas_call(
        functools.partial(unpack_kernel, n, count),
        out_shape=(shape,) * count,
        in_specs=[pl.BlockSpec(memory_space=VMEM)] * n,
        out_specs=(pl.BlockSpec(memory_space=pl.ANY),) * count,
        scratch_shapes=[pltpu.SemaphoreType.DMA],
        compiler_params=pltpu.CompilerParams(vmem_limit_bytes=8 * MIB),
        name="unpack",
    )(*[in_vmem(c) for c in chunks])


def dot_t(a, b):
    return lax.dot_general(a, b, (((1,), (1,)), ((), ())), preferred_element_type=jnp.float32)


def t_dot(a, b):
    return lax.dot_general(a, b, (((0,), (0,)), ((), ())), preferred_element_type=jnp.float32)


def attention_kernel(n, tok, mem, *refs):
    ins, (bias_ref, pass_ref), outs, dbias_ref = refs[:n], refs[n : n + 2], refs[n + 2 : 2 * n + 2], refs[2 * n + 2]
    qs, gs, kpad, vpad, mem_k, mem_v, dqs, dk_acc, dv_acc = refs[2 * n + 3 :]
    width = ins[0].shape[1]
    length = n * tok
    step = 2 * tok
    scale = 1.0 / math.sqrt(width)
    me = lax.axis_index("seq")
    zeros = jnp.zeros((step, width), kpad.dtype)
    kpad[0:step, :] = zeros
    vpad[0:step, :] = zeros
    bias = bias_ref[...]
    for i, (o, ref) in enumerate(zip(offsets(n), ins, strict=True)):
        lo = pl.multiple_of((me ^ o) * tok, tok)
        own = pl.ds(lo, tok)
        later = pl.ds(pl.multiple_of(lo + step, tok), tok)
        qs[own, :] = (ref[0:tok, :].astype(jnp.float32) + bias).astype(qs.dtype)
        gs[own, :] = ref[tok : 2 * tok, :]
        kpad[later, :] = ref[2 * tok : 3 * tok, :]
        vpad[later, :] = ref[3 * tok : 4 * tok, :]
        mem_k[i * mem : (i + 1) * mem, :] = ref[4 * tok : 4 * tok + mem, :]
        mem_v[i * mem : (i + 1) * mem, :] = ref[4 * tok + mem : 4 * tok + 2 * mem, :]
    dk_acc[...] = jnp.zeros_like(dk_acc)
    dv_acc[...] = jnp.zeros_like(dv_acc)
    rows = lax.broadcasted_iota(jnp.int32, (step, step), 0)
    cols = lax.broadcasted_iota(jnp.int32, (step, step), 1)
    causal = cols <= rows
    total = jnp.zeros((1, width), jnp.float32)
    ids_before = jnp.full((step, step), -1, jnp.int32)
    for c in range(length // step):
        lo = c * step
        ids = jnp.broadcast_to(pass_ref[:, lo : lo + step], (step, step))
        ids_q = ids.T
        seen = jnp.concatenate([ids_q == ids_before, (ids_q == ids) & causal], axis=1)
        ids_before = ids
        q = qs[lo : lo + step, :]
        g = gs[lo : lo + step, :]
        k_loc = kpad[lo : lo + 2 * step, :]
        v_loc = vpad[lo : lo + 2 * step, :]
        raw_m = dot_t(q, mem_k[...])
        raw_l = jnp.where(seen, dot_t(q, k_loc), -jnp.inf)
        top = jnp.maximum(jnp.max(raw_m, axis=1, keepdims=True), jnp.max(raw_l, axis=1, keepdims=True))
        e_m = jnp.exp2((raw_m - top) * (scale * LOG2E))
        e_l = jnp.exp2((raw_l - top) * (scale * LOG2E))
        norm = jnp.sum(e_m, axis=1, keepdims=True) + jnp.sum(e_l, axis=1, keepdims=True)
        inv = 1.0 / norm
        w_m = e_m * inv
        w_l = e_l * inv
        wb_m = w_m.astype(jnp.bfloat16)
        wb_l = w_l.astype(jnp.bfloat16)
        vd_m = dot_t(g, mem_v[...])
        vd_l = dot_t(g, v_loc)
        delta = jnp.sum(wb_m.astype(jnp.float32) * vd_m, axis=1, keepdims=True) + jnp.sum(
            wb_l.astype(jnp.float32) * vd_l, axis=1, keepdims=True
        )
        ds_m = (w_m * (vd_m - delta) * scale).astype(jnp.bfloat16)
        ds_l = (w_l * (vd_l - delta) * scale).astype(jnp.bfloat16)
        dq = jnp.dot(ds_m, mem_k[...], preferred_element_type=jnp.float32) + jnp.dot(
            ds_l, k_loc, preferred_element_type=jnp.float32
        )
        total = total + jnp.sum(dq, axis=0, keepdims=True)
        dqs[lo : lo + step, :] = dq.astype(dqs.dtype)
        dk_acc[lo : lo + 2 * step, :] += t_dot(ds_l, q)
        dv_acc[lo : lo + 2 * step, :] += t_dot(wb_l, g)
    for o, out in zip(offsets(n), outs, strict=True):
        lo = pl.multiple_of((me ^ o) * tok, tok)
        later = pl.ds(pl.multiple_of(lo + step, tok), tok)
        out[0:tok, :] = dqs[pl.ds(lo, tok), :]
        out[tok : 2 * tok, :] = dk_acc[later, :].astype(out.dtype)
        out[2 * tok : 3 * tok, :] = dv_acc[later, :].astype(out.dtype)
    dbias_ref[...] = total / length


def attention(chunks, bias, passages, tok, mem):
    n, width = len(chunks), bias.shape[1]
    dtype = chunks[0].dtype
    length = n * tok
    pad = length + 2 * tok
    flops = 2 * length * width * (3 * n * mem + 5 * 4 * tok)
    *grads, d_bias = pl.pallas_call(
        functools.partial(attention_kernel, n, tok, mem),
        out_shape=(VMEM((3 * tok, width), dtype),) * n + (VMEM((1, width), jnp.float32),),
        in_specs=[pl.BlockSpec(memory_space=VMEM)] * (n + 2),
        out_specs=(pl.BlockSpec(memory_space=VMEM),) * (n + 1),
        scratch_shapes=[
            VMEM((length, width), dtype),
            VMEM((length, width), dtype),
            VMEM((pad, width), dtype),
            VMEM((pad, width), dtype),
            VMEM((n * mem, width), dtype),
            VMEM((n * mem, width), dtype),
            VMEM((length, width), dtype),
            VMEM((pad, width), jnp.float32),
            VMEM((pad, width), jnp.float32),
        ],
        cost_estimate=pl.CostEstimate(
            flops=flops, bytes_accessed=length * width * 32, transcendentals=length * (n * mem + 4 * tok)
        ),
        compiler_params=pltpu.CompilerParams(vmem_limit_bytes=32 * MIB),
        name="attention",
    )(*[in_vmem(c) for c in chunks], bias, passages)
    return grads, d_bias


def sum_over(x, axis, size):
    reach = 1
    while reach < size:
        x = x + lax.ppermute(x, axis, [(s, s ^ reach) for s in range(size)])
        reach *= 2
    return x


def body(n, copies, queries, key_rows, value_rows, out_grad, mem_keys, mem_values, content_bias, passage_ids):
    tok, mem = queries.shape[1], mem_keys.shape[1]
    width = content_bias.shape[1]
    sent = pack((queries, out_grad, key_rows, value_rows, mem_keys, mem_values), n, width)
    grads, d_bias = attention(exchange(sent, n), content_bias, passage_ids, tok, mem)
    d_queries, d_keys, d_values = unpack(exchange(grads, n), 3, n, width)
    return (d_queries, d_keys, d_values, sum_over(d_bias, "dp", copies))


def solution(mesh):
    rows = P("dp", "seq", None)
    return jax.shard_map(
        functools.partial(body, mesh.shape["seq"], mesh.shape["dp"]),
        mesh=mesh,
        in_specs=(rows,) * 6 + (P("seq", None), P("dp", None)),
        out_specs=(rows,) * 3 + (P("seq", None),),
        check_vma=False,
    )
```
